128 devices in a mesh: row: 16 (over z, y), col: 8 (over x, core).
Axes of the slice: x: 4, y: 4, z: 4, core: 2. Of those that a mesh axis runs over, the one named last changes fastest.
Arguments:
- attn_in: bfloat16 [512, 16384], P('row', 'col'), may hold values from -6 to 6
- w_out: bfloat16 [16384, 16384], P('col', 'row'), may hold values from -0.046875 to 0.046875
- resid: bfloat16 [512, 16384], P('col', 'row'), may hold values from -64 to 64, as said below
- norm_gain: float32 [16384], P('row'), may hold values from 0.1 to 1.9
- w_gate: bfloat16 [16384, 26624], P('row', 'col'), may hold values from -0.046875 to 0.046875
- w_up: bfloat16 [16384, 26624], P('row', 'col'), may hold values from -0.046875 to 0.046875
- w_down: bfloat16 [26624, 16384], P('col', 'row'), may hold values from -0.0390625 to 0.0390625
Outputs:
- layer_out: bfloat16 [512, 16384], P('col', 'row')
The draws below stay inside these ranges and needn't reach their ends.
Inputs may be any that keep to these rules, and one draw needn't show every extreme that they name: `resid`: entries are real-valued and not all of one size.
All inputs are finite; a program needn't handle non-finite values.
Results may differ from the reference program's by a relative error of at most 0.0051.
Values may be sent and summed in bfloat16 or wider, within the bound.
No kernel may reach another device: no remote copies, remote signals or barrier semaphores. Data moves between devices by JAX's collectives and lax.ppermute only.
A program may use at most 128 MiB of HBM per device.

```python
import jax
import jax.numpy as jnp
from jax import lax

D = 16384
FF = 26624
TOKENS = 512


def draw_resid(key, part):
    k_base = jax.random.fold_in(key, 11)
    k_rows = jax.random.fold_in(key, 12)
    k_cols = jax.random.fold_in(key, 13)
    column = jnp.arange(D, dtype=jnp.float32) / D
    ramp = jnp.exp(0.5 * jnp.log(3.0) * column)
    col_scale = jnp.exp(jax.random.uniform(k_cols, (D,), jnp.float32, jnp.log(0.5), jnp.log(3.0))) * ramp
    row_scale = jnp.exp(jax.random.uniform(k_rows, (TOKENS, 1), jnp.float32, jnp.log(0.3), jnp.log(3.0)))
    base = jnp.clip(jax.random.normal(k_base, (TOKENS, D), jnp.float32), -4.0, 4.0)
    values = base * row_scale * col_scale[None, :]
    return jnp.clip(values, -64.0, 64.0).astype(jnp.bfloat16)


def steps_of(own_key, shape, split, smallest, largest):
    loudness, own = 1.0, jax.random.fold_in(own_key, 6)
    for position, blocks in split:
        draws = jnp.exp(jax.random.uniform(jax.random.fold_in(own, position), (blocks,), jnp.float32, smallest / len(split), largest / len(split)))
        loudness = loudness * jnp.repeat(draws, shape[position] // blocks).reshape([-1 if axis == position else 1 for axis in range(len(shape))])
    return loudness


def centred(key, dims, spread, limit, split=(), kind=jnp.bfloat16):
    entries = jax.random.normal(key, dims, jnp.float32) * spread
    if len(split) > 0:
        entries = steps_of(key, dims, split, -0.22, 0.18) * entries
    return jnp.clip(entries, min=-limit, max=limit).astype(kind)


def setup_inputs(seed: int = 0) -> dict:
    keys = jax.random.split(jax.random.key(seed), 8)
    return {
        "attn_in": centred(keys[0], (TOKENS, D), 1.0, 6.0, ((0, 16), (1, 8))),
        "w_out": centred(keys[1], (D, D), D ** -0.5, 0.046875, ((0, 8), (1, 16))),
        "resid": draw_resid(jax.random.fold_in(keys[7], 71), 0),
        "norm_gain": jnp.clip(1.0 + 0.18 * jax.random.normal(keys[3], (D,), jnp.float32), 0.1, 1.9),
        "w_gate": centred(keys[4], (D, FF), D ** -0.5, 0.046875, ((0, 16), (1, 8))),
        "w_up": centred(keys[5], (D, FF), D ** -0.5, 0.046875, ((0, 16), (1, 8))),
        "w_down": centred(keys[6], (FF, D), FF ** -0.5, 0.0390625, ((0, 8), (1, 16))),
    }


def reference(attn_in, w_out, resid, norm_gain, w_gate, w_up, w_down):
    projected = jnp.dot(attn_in, w_out, preferred_element_type=jnp.float32)
    stream = (resid.astype(jnp.float32) + projected).astype(jnp.bfloat16)
    stream_f = stream.astype(jnp.float32)
    mean_square = lax.optimization_barrier(jnp.mean(stream_f * stream_f, axis=1, keepdims=True))
    normed = (stream_f * lax.rsqrt(mean_square + 1e-05) * norm_gain[None, :]).astype(jnp.bfloat16)
    gate = jnp.dot(normed, w_gate, preferred_element_type=jnp.float32)
    up_part = jnp.dot(normed, w_up, preferred_element_type=jnp.float32)
    activated = (jax.nn.silu(gate) * up_part).astype(jnp.bfloat16)
    down = jnp.dot(activated, w_down, preferred_element_type=jnp.float32)
    return (stream_f + down).astype(jnp.bfloat16)
```

```python
import jax
import jax.numpy as jnp
from jax import lax
from jax.experimental import pallas as pl
from jax.experimental.pallas import tpu as pltpu
from jax.sharding import PartitionSpec as P

D = 16384
EPS = 1e-05
BF = jnp.bfloat16
F32 = jnp.float32


def y_send(v, k):
    return lax.ppermute(v, "row", [(z * 4 + y, z * 4 + (y + k) % 4) for z in range(4) for y in range(4)])


def z_send(v, k):
    return lax.ppermute(v, "row", [(z * 4 + y, (z + k) % 4 * 4 + y) for z in range(4) for y in range(4)])


def x_send(v, k):
    return lax.ppermute(v, "col", [(x * 2 + c, (x + k) % 4 * 2 + c) for x in range(4) for c in range(2)])


def swap(v):
    return lax.ppermute(v, "col", [(i, i ^ 1) for i in range(8)])


def gather4(v, send):
    return [v, send(v, 1), send(v, 2), send(v, 3)]


def two_axis_gather(v, first, second):
    near = jnp.concatenate(gather4(v, first), axis=0)
    return gather4(near, second)


def vmem(shape):
    return pl.BlockSpec(shape, lambda i, s: (0,) * len(shape))


def assembled_matmul(spots, ones, twos, w, tn=256):
    half = ones[0].shape[1]
    n = w.shape[1]

    def kernel(spot, *refs):
        a, b, w_ref, keep, away, lhs = refs[:4], refs[4:8], *refs[8:]

        @pl.when(pl.program_id(0) == 0)
        def _():
            for kz in range(4):
                for ky in range(4):
                    rows = pl.ds(pl.multiple_of(spot[4 * kz + ky] * 32, 32), 32)
                    lhs[rows, :half] = a[kz][ky * 32 : ky * 32 + 32, :]
                    lhs[rows, half:] = b[ky][kz * 32 : kz * 32 + 32, :]

        out = jnp.dot(lhs[...], w_ref[...], preferred_element_type=F32)
        keep[...] = out[:256]
        away[...] = out[256:].astype(BF)

    return pl.pallas_call(
        kernel,
        out_shape=(jax.ShapeDtypeStruct((256, n), F32), jax.ShapeDtypeStruct((256, n), BF)),
        grid_spec=pltpu.PrefetchScalarGridSpec(
            num_scalar_prefetch=1,
            grid=(n // tn,),
            in_specs=[vmem((128, half))] * 8 + [pl.BlockSpec((2 * half, tn), lambda i, s: (0, i))],
            out_specs=[pl.BlockSpec((256, tn), lambda i, s: (0, i))] * 2,
            scratch_shapes=[pltpu.VMEM((512, 2 * half), BF)],
        ),
    )(spots, *ones, *twos, w)


def gate_matmul(spots, mine, partners, gain, w, tn=256):
    n = w.shape[1]
    steps = n // tn

    def kernel(spot, s0, s1, g_ref, w_ref, far_a, far_b, right, left, own, lhs, squares):
        i = pl.program_id(0)

        @pl.when(i == 0)
        def _():
            for b in range(16):
                src = s0 if b < 8 else s1
                v = src[b % 8 * 32 : b % 8 * 32 + 32, :].astype(F32)
                rows = pl.ds(pl.multiple_of(spot[b] * 32, 32), 32)
                lhs[rows, :] = (v * g_ref[...]).astype(BF)
                v2 = v * v
                squares[rows, :] = sum(v2[:, j * 128 : j * 128 + 128] for j in range(8))

        def put(v, width):
            v = v.astype(BF)
            own[:, :width] = v[:128]
            right[:, :width] = v[128:256]
            far_a[:, :width] = v[256:320]
            far_b[:, :width] = v[320:384]
            left[:, :width] = v[384:]

        @pl.when(i < steps)
        def _():
            put(jnp.dot(lhs[...], w_ref[...], preferred_element_type=F32), tn)

        @pl.when(i == steps)
        def _():
            put(squares[...], 128)

    rows = (64, 64, 128, 128, 128)
    return pl.pallas_call(
        kernel,
        out_shape=[jax.ShapeDtypeStruct((r, n + 128), BF) for r in rows] + [jax.ShapeDtypeStruct((512, w.shape[0]), BF)],
        grid_spec=pltpu.PrefetchScalarGridSpec(
            num_scalar_prefetch=1,
            grid=(steps + 1,),
            in_specs=[vmem((256, w.shape[0]))] * 2
            + [vmem((1, w.shape[0])), pl.BlockSpec((w.shape[0], tn), lambda i, s: (0, jnp.minimum(i, steps - 1)))],
            out_specs=[pl.BlockSpec((r, tn), lambda i, s: (0, i)) for r in rows] + [vmem((512, w.shape[0]))],
            scratch_shapes=[pltpu.VMEM((512, 128), F32)],
        ),
    )(spots, mine, partners, gain, w)


def up_matmul(lhs, w, tn=256):
    n = w.shape[1]

    def kernel(l_ref, w_ref, far_a, far_b, right, left, own):
        out = jnp.dot(l_ref[...], w_ref[...], preferred_element_type=F32).astype(BF)

        def piece(ky, kz):
            p = (4 * ky + kz) * 32
            return out[p : p + 32]

        for ky in range(4):
            rows = pl.ds(ky * 32, 32)
            own[rows, :] = piece(ky, 0)
            right[rows, :] = piece(ky, 1)
            left[rows, :] = piece(ky, 3)
            (far_a if ky < 2 else far_b)[pl.ds(ky % 2 * 32, 32), :] = piece(ky, 2)

    rows = (64, 64, 128, 128, 128)
    return pl.pallas_call(
        kernel,
        out_shape=[jax.ShapeDtypeStruct((r, n), BF) for r in rows],
        grid=(n // tn,),
        in_specs=[pl.BlockSpec(lhs.shape, lambda i: (0, 0)), pl.BlockSpec((w.shape[0], tn), lambda i: (0, i))],
        out_specs=[pl.BlockSpec((r, tn), lambda i: (0, i)) for r in rows],
    )(lhs, w)


def add(a, b):
    return a.astype(F32) + b.astype(F32)


def two_axis_sum(blocks, first, second):
    far_a, far_b, right, left, own = blocks
    from_before = first(far_a, 1)
    from_after = first(far_b, 3)
    right = jnp.concatenate([add(right[:64], from_before).astype(BF), right[64:]], axis=0)
    left = jnp.concatenate([left[:64], add(left[64:], from_after).astype(BF)], axis=0)
    total = add(own, first(right, 1)) + first(left, 3).astype(F32)
    mine = total[:32]
    parts = [second(total[k * 32 : k * 32 + 32].astype(BF), k) for k in (1, 2, 3)]
    return mine + sum(p.astype(F32) for p in parts)


def column_sum(keep, away, sign):
    both = keep + swap(away).astype(F32)
    parts = [x_send(both[k * 64 : k * 64 + 64].astype(BF), sign * k) for k in (1, 2, 3)]
    return both[:64] + sum(p.astype(F32) for p in parts)


def on_device(attn_in, w_out, resid, norm_gain, w_gate, w_up, w_down):
    row, col = lax.axis_index("row"), lax.axis_index("col")
    z, y, x, core = row // 4, row % 4, col // 2, col % 2
    k_hi, k_lo = jnp.arange(16, dtype=jnp.int32) // 4, jnp.arange(16, dtype=jnp.int32) % 4

    half = attn_in.shape[1] // 2
    ones = two_axis_gather(attn_in[:, :half], y_send, z_send)
    twos = two_axis_gather(attn_in[:, half:], z_send, y_send)
    zb, yb = (z - k_hi) % 4, (y - k_lo) % 4
    spots = (yb // 2 ^ core) * 8 + (zb - x) % 4 * 2 + yb % 2
    keep, away = assembled_matmul(spots.astype(jnp.int32), ones, twos, w_out)
    projected = column_sum(keep, away, 1)

    stream = (resid.astype(F32) + projected).astype(BF)
    mine = jnp.concatenate(gather4(stream, x_send), axis=0)
    partners = swap(mine)

    spots = (k_hi - y) % 4 * 4 + (k_lo - z) % 4
    *gate_blocks, lhs = gate_matmul(spots.astype(jnp.int32), mine, partners, norm_gain[None, :], w_gate)
    up_blocks = up_matmul(lhs, w_up)
    gate_sum = two_axis_sum(gate_blocks, y_send, z_send)
    up = two_axis_sum(up_blocks, z_send, y_send)

    width = w_gate.shape[1]
    mean_square = jnp.sum(gate_sum[:, width:], axis=1, keepdims=True) / D
    scale = lax.rsqrt(mean_square + EPS)
    activated = (jax.nn.silu(gate_sum[:, :width] * scale) * (up * scale)).astype(BF)

    half = width // 2
    ones = two_axis_gather(activated[:, :half], y_send, z_send)
    twos = two_axis_gather(activated[:, half:], z_send, y_send)
    spots = (y - k_lo) % 4 * 4 + (z - k_hi) % 4
    keep, away = assembled_matmul(spots.astype(jnp.int32), ones, twos, w_down)
    down = column_sum(keep, away, -1)
    return (stream.astype(F32) + down).astype(BF)


def solution(mesh):
    placed = (
        P("row", "col"),
        P("col", "row"),
        P("col", "row"),
        P("row"),
        P("row", "col"),
        P("row", "col"),
        P("col", "row"),
    )
    return jax.shard_map(
        on_device, mesh=mesh, in_specs=placed, out_specs=P("col", "row"), check_vma=False
    )
```

```python
import jax
import jax.numpy as jnp
from jax import lax
from jax.experimental import pallas as pl
from jax.experimental.pallas import tpu as pltpu
from jax.sharding import PartitionSpec as P


D = 16384
EPS = 1e-05
BF = jnp.bfloat16
F32 = jnp.float32


def y_send(v, k):
    return lax.ppermute(v, "row", [(z * 4 + y, z * 4 + (y + k) % 4) for z in range(4) for y in range(4)])


def z_send(v, k):
    return lax.ppermute(v, "row", [(z * 4 + y, (z + k) % 4 * 4 + y) for z in range(4) for y in range(4)])


def x_send(v, k):
    return lax.ppermute(v, "col", [(x * 2 + c, (x + k) % 4 * 2 + c) for x in range(4) for c in range(2)])


def swap(v):
    return lax.ppermute(v, "col", [(i, i ^ 1) for i in range(8)])


def gather4(v, send):
    return [v, send(v, 1), send(v, 2), send(v, 3)]


def two_axis_gather(v, first, second):
    near = jnp.concatenate(gather4(v, first), axis=0)
    return gather4(near, second)


HERE = pl.BlockSpec(memory_space=pltpu.VMEM)
SCALARS = pl.BlockSpec(memory_space=pltpu.SMEM)
TILE = 256


def near(v):
    return pltpu.with_memory_space_constraint(v, pltpu.VMEM)


def call(kernel, outs, *args, scalars=None, scratch=(), flops=0):
    specs = [HERE] * len(args)
    args = [near(v) for v in args]
    if scalars is not None:
        specs, args = [SCALARS] + specs, [scalars] + args
    return pl.pallas_call(
        kernel,
        out_shape=[pltpu.VMEM(*o) for o in outs],
        in_specs=specs,
        out_specs=[HERE] * len(outs),
        scratch_shapes=scratch,
        compiler_params=pltpu.CompilerParams(vmem_limit_bytes=6 << 20),
        cost_estimate=pl.CostEstimate(flops=flops, bytes_accessed=1 << 20, transcendentals=0),
    )(*args)


def load(*weights):
    count = len(weights)

    def kernel(*refs):
        sems = refs[-1]
        copies = [pltpu.make_async_copy(refs[i], refs[count + i], sems.at[i]) for i in range(count)]
        for copy in copies:
            copy.start()
        for copy in copies:
            copy.wait()

    return pl.pallas_call(
        kernel,
        out_shape=[pltpu.VMEM(w.shape, w.dtype) for w in weights],
        in_specs=[pl.BlockSpec(memory_space=pltpu.HBM)] * count,
        out_specs=[HERE] * count,
        scratch_shapes=[pltpu.SemaphoreType.DMA((count,))],
        compiler_params=pltpu.CompilerParams(vmem_limit_bytes=1 << 20),
        cost_estimate=pl.CostEstimate(flops=0, bytes_accessed=2 * sum(w.size for w in weights), transcendentals=0),
    )(*(pltpu.with_memory_space_constraint(w, pltpu.HBM) for w in weights))


def dot(a, b):
    return jnp.dot(a, b, preferred_element_type=F32)


def assembled_matmul(spots, ones, twos, w):
    half = ones[0].shape[1]
    k, n = w.shape

    def last_rows(spot, *refs):
        a, b, w_ref, lhs, away = refs[:4], refs[4:8], *refs[8:]
        for kz in range(4):
            for ky in range(4):
                rows = pl.ds(pl.multiple_of(spot[4 * kz + ky] * 32, 32), 32)
                lhs[rows, :half] = a[kz][ky * 32 : ky * 32 + 32, :]
                lhs[rows, half:] = b[ky][kz * 32 : kz * 32 + 32, :]
        for i in range(0, n, TILE):
            away[:, i : i + TILE] = dot(lhs[256:, :], w_ref[:, i : i + TILE]).astype(BF)

    def first_rows(lhs, w_ref, keep):
        for i in range(0, n, TILE):
            keep[:, i : i + TILE] = dot(lhs[:256, :], w_ref[:, i : i + TILE])

    cost = 2 * 256 * k * n
    lhs, away = call(last_rows, [((512, k), BF), ((256, n), BF)], *ones, *twos, w, scalars=spots, flops=cost)
    (keep,) = call(first_rows, [((256, n), F32)], lhs, w, flops=cost)
    return keep, away


def gate_far(spots, mine, partners, gain, w):
    k, n = w.shape

    def kernel(spot, s0, s1, g_ref, w_ref, lhs, squares, far_a, far_b):
        for b in range(16):
            src = s0 if b < 8 else s1
            v = src[b % 8 * 32 : b % 8 * 32 + 32, :].astype(F32)
            rows = pl.ds(pl.multiple_of(spot[b] * 32, 32), 32)
            lhs[rows, :] = (v * g_ref[...]).astype(BF)
            v2 = v * v
            squares[rows, :] = sum(v2[:, j * 128 : j * 128 + 128] for j in range(k // 128)).astype(BF)
        for i in range(0, n, TILE):
            out = dot(lhs[256:384, :], w_ref[:, i : i + TILE]).astype(BF)
            far_a[:, i : i + TILE] = out[:64]
            far_b[:, i : i + TILE] = out[64:]
        far_a[:, n:] = squares[256:320, :]
        far_b[:, n:] = squares[320:384, :]

    outs = [((512, k), BF), ((512, 128), BF), ((64, n + 128), BF), ((64, n + 128), BF)]
    return call(kernel, outs, mine, partners, gain, w, scalars=spots, flops=2 * 128 * k * n)


def gate_near(lhs, squares, w):
    k, n = w.shape

    def kernel(l_ref, q_ref, w_ref, right, left, own):
        for i in range(0, n, TILE):
            cols = slice(i, i + TILE)
            out = dot(l_ref[:256, :], w_ref[:, cols]).astype(BF)
            own[:, cols] = out[:128]
            right[:, cols] = out[128:]
            left[:, cols] = dot(l_ref[384:, :], w_ref[:, cols]).astype(BF)
        own[:, n:] = q_ref[:128, :]
        right[:, n:] = q_ref[128:256, :]
        left[:, n:] = q_ref[384:, :]

    return call(kernel, [((128, n + 128), BF)] * 3, lhs, squares, w, flops=2 * 384 * k * n)


def up_far(lhs, w):
    k, n = w.shape

    def kernel(l_ref, w_ref, far_a, far_b):
        left_side = jnp.concatenate([l_ref[p * 128 + 64 : p * 128 + 96, :] for p in range(4)], axis=0)
        for i in range(0, n, TILE):
            out = dot(left_side, w_ref[:, i : i + TILE]).astype(BF)
            far_a[:, i : i + TILE] = out[:64]
            far_b[:, i : i + TILE] = out[64:]

    return call(kernel, [((64, n), BF)] * 2, lhs, w, flops=2 * 128 * k * n)


def up_near(lhs, w):
    k, n = w.shape

    def kernel(l_ref, w_ref, right, left, own, side):
        for p in range(4):
            for q, kz in enumerate((0, 1, 3)):
                side[q * 128 + p * 32 : q * 128 + p * 32 + 32, :] = l_ref[p * 128 + kz * 32 : p * 128 + kz * 32 + 32, :]
        for i in range(0, n, TILE):
            cols = slice(i, i + TILE)
            out = dot(side[:256, :], w_ref[:, cols]).astype(BF)
            own[:, cols] = out[:128]
            right[:, cols] = out[128:]
            left[:, cols] = dot(side[256:, :], w_ref[:, cols]).astype(BF)

    scratch = [pltpu.VMEM((384, k), BF)]
    return call(kernel, [((128, n), BF)] * 3, lhs, w, scratch=scratch, flops=2 * 384 * k * n)


def add(a, b):
    return a.astype(F32) + b.astype(F32)


def two_axis_sum(blocks, first, second):
    far_a, far_b, right, left, own = blocks
    from_before = first(far_a, 1)
    from_after = first(far_b, 3)
    right = jnp.concatenate([add(right[:64], from_before).astype(BF), right[64:]], axis=0)
    left = jnp.concatenate([left[:64], add(left[64:], from_after).astype(BF)], axis=0)
    right = first(right, 1)
    left = first(left, 3)
    total = add(own, right) + left.astype(F32)
    mine = total[:32]
    parts = [total[k * 32 : k * 32 + 32].astype(BF) for k in (1, 2, 3)]
    parts = [second(p, k) for k, p in zip((1, 2, 3), parts)]
    return mine + sum(p.astype(F32) for p in parts)


def column_sum(keep, away, sign):
    both = keep + swap(away).astype(F32)
    parts = [x_send(both[k * 64 : k * 64 + 64].astype(BF), sign * k) for k in (1, 2, 3)]
    return both[:64] + sum(p.astype(F32) for p in parts)


def layer(attn_in, w_out, resid, norm_gain, w_gate, w_up, w_down):
    row, col = lax.axis_index("row"), lax.axis_index("col")
    z, y, x, core = row // 4, row % 4, col // 2, col % 2
    k_hi, k_lo = jnp.arange(16, dtype=jnp.int32) // 4, jnp.arange(16, dtype=jnp.int32) % 4

    w_out, w_gate, w_up, w_down = load(w_out, w_gate, w_up, w_down)
    half = attn_in.shape[1] // 2
    ones = two_axis_gather(attn_in[:, :half], y_send, z_send)
    twos = two_axis_gather(attn_in[:, half:], z_send, y_send)
    zb, yb = (z - k_hi) % 4, (y - k_lo) % 4
    spots = (yb // 2 ^ core) * 8 + (zb - x) % 4 * 2 + yb % 2
    keep, away = assembled_matmul(spots.astype(jnp.int32), ones, twos, w_out)
    projected = column_sum(keep, away, 1)

    stream = (resid.astype(F32) + projected).astype(BF)
    mine = jnp.concatenate(gather4(stream, x_send), axis=0)
    partners = swap(mine)

    spots = (k_hi - y) % 4 * 4 + (k_lo - z) % 4
    lhs, squares, *gate_away = gate_far(spots.astype(jnp.int32), mine, partners, norm_gain[None, :], w_gate)
    up_away = up_far(lhs, w_up)
    near_gate = gate_near(lhs, squares, w_gate)
    near_up = up_near(lhs, w_up)
    gate_sum = two_axis_sum((*gate_away, *near_gate), y_send, z_send)
    up = two_axis_sum((*up_away, *near_up), z_send, y_send)

    width = w_gate.shape[1]
    mean_square = jnp.sum(gate_sum[:, width:], axis=1, keepdims=True) / D
    scale = lax.rsqrt(mean_square + EPS)
    activated = (jax.nn.silu(gate_sum[:, :width] * scale) * (up * scale)).astype(BF)

    half = width // 2
    ones = two_axis_gather(activated[:, :half], y_send, z_send)
    twos = two_axis_gather(activated[:, half:], z_send, y_send)
    spots = (y - k_lo) % 4 * 4 + (z - k_hi) % 4
    keep, away = assembled_matmul(spots.astype(jnp.int32), ones, twos, w_down)
    down = column_sum(keep, away, -1)
    return (stream.astype(F32) + down).astype(BF)


def solution(mesh):
    placed = (
        P("row", "col"),
        P("col", "row"),
        P("col", "row"),
        P("row"),
        P("row", "col"),
        P("row", "col"),
        P("col", "row"),
    )
    return jax.shard_map(layer, mesh=mesh, in_specs=placed, out_specs=P("col", "row"), check_vma=False)
```
